512 devices in a mesh: row: 16 (over y_hi, x), col: 32 (over z, y_lo, core).
Axes of the slice: x: 4, y: 8 (y_hi: 4, y_lo: 2; y = y_hi * 2 + y_lo), z: 8, core: 2. Of those that a mesh axis runs over, the one named last changes fastest.
Arguments:
- query: bfloat16 [16384, 1024], P(('row', 'col')), may hold values from -0.5375 to 0.5375
- passage: bfloat16 [16384, 1024], P(('row', 'col')), may hold values from -0.43 to 0.43
- positive: int32 [512, 32], P(('row', 'col')), may hold values from 0 to 31, each once within a row
Outputs:
- loss_value: float32 [], replicated
- grad_query: bfloat16 [16384, 1024], P(('row', 'col'))
- grad_passage: bfloat16 [16384, 1024], P(('row', 'col'))
The draws below stay inside these ranges and needn't reach their ends.
Inputs may be any that keep to these rules, and one draw needn't show every extreme that they name: Each row of positive names every position 0 to 31 once.
All inputs are finite; a program needn't handle non-finite values.
Results may differ from the reference program's by a relative error of at most 0.015.
Values may be sent and summed in bfloat16 or wider, within the bound.
No kernel may reach another device: no remote copies, remote signals or barrier semaphores. Data moves between devices by JAX's collectives and lax.ppermute only.
A program may use at most 64 MiB of HBM per device.

```python
import jax
import jax.numpy as jnp
from jax import lax

EMBED = 1024
ROWS_DEV = 32
BLOCKS = 512
BATCH = 16384
N_ROW = 16
N_COL = 32


emb_scale = 0.07


def drawn_rows(key):
    row_index = jnp.arange(BATCH, dtype=jnp.int32)
    shard_index = row_index // ROWS_DEV
    pattern = jax.random.uniform(jax.random.fold_in(key, 37), (BATCH, EMBED), jnp.float32, -1.0, 1.0)
    level = 150.0 + 80.0 * (shard_index % 2).astype(jnp.float32) + 10.0 * (shard_index // 2 % 3).astype(jnp.float32)
    amplitude = jnp.sqrt(level * 3.0 / (20.0 * EMBED))
    return (row_index, pattern, amplitude)


def draw_passage(key, part):
    subkey = jax.random.fold_in(key, 11)
    values = jax.random.truncated_normal(subkey, -6.0, 6.0, (BATCH, EMBED), jnp.float32) * emb_scale
    row_index, pattern, amplitude = drawn_rows(key)
    own_aligned = row_index % ROWS_DEV == 0
    partner_aligned = row_index % ROWS_DEV == 1
    own_values = amplitude[:, None] * pattern
    partner_values = 0.99 * own_values[row_index ^ 1]
    values = jnp.where(own_aligned[:, None], own_values, jnp.where(partner_aligned[:, None], partner_values, values))
    return values.astype(jnp.bfloat16)


def draw_query(key, part):
    subkey = jax.random.fold_in(key, 23)
    row_index, pattern, amplitude = drawn_rows(key)
    shard_index = row_index // ROWS_DEV
    shard_pos = shard_index.astype(jnp.float32) / (BLOCKS - 1.0)
    parity = (shard_index % 2).astype(jnp.float32)
    spread = (1.0 + 2.0 * shard_pos) * (1.0 + parity)
    sigma = spread / (20.0 * emb_scale * jnp.sqrt(EMBED * 1.0))
    values = jax.random.truncated_normal(subkey, -4.0, 4.0, (BATCH, EMBED), jnp.float32) * sigma[:, None]
    aligned = row_index % ROWS_DEV == 0
    values = jnp.where(aligned[:, None], amplitude[:, None] * pattern, values)
    return values.astype(jnp.bfloat16)


def setup_inputs(seed: int = 0) -> dict:
    key_of = jax.random.split(jax.random.key(seed), 4)
    return {
        "query": draw_query(jax.random.fold_in(key_of[3], 71), 0),
        "passage": draw_passage(jax.random.fold_in(key_of[3], 71), 0),
        "positive": jax.vmap(lambda own: jax.random.permutation(own, ROWS_DEV))(jax.random.split(key_of[2], BLOCKS)).reshape((BLOCKS, ROWS_DEV)).astype(jnp.int32),
    }


logit_scale = 20.0


def reference(query, passage, positive):
    paired_index = (jnp.arange(BLOCKS, dtype=jnp.int32)[:, None] * ROWS_DEV + positive.astype(jnp.int32)).reshape(BATCH)
    query_groups = query.reshape(N_ROW, N_COL * ROWS_DEV, EMBED)
    passage_groups = passage.reshape(N_ROW, N_COL, ROWS_DEV, EMBED).transpose(1, 0, 2, 3).reshape(N_COL, N_ROW * ROWS_DEV, EMBED)

    def tile_scores(query_rows):
        return logit_scale * jnp.dot(query_rows, passage.T, preferred_element_type=jnp.float32)

    def first_sweep(carry, query_rows):
        old_peak, old_total = carry
        scores = tile_scores(query_rows)
        row_lse = jax.nn.logsumexp(scores, axis=1)
        new_peak = jnp.maximum(old_peak, scores.max(axis=0))
        new_total = old_total * jnp.exp(old_peak - new_peak) + jnp.exp(scores - new_peak[None, :]).sum(axis=0)
        return (new_peak, new_total), row_lse

    start_peak = jnp.full((BATCH,), -1e30, jnp.float32)
    start_total = jnp.zeros((BATCH,), jnp.float32)
    (col_peak, col_total), row_lse = lax.scan(first_sweep, (start_peak, start_total), query_groups)
    col_lse = col_peak + jnp.log(col_total)

    def second_sweep(passage_acc, inputs):
        query_rows, row_part = inputs
        scores = tile_scores(query_rows)
        weights = (0.5 * (jnp.exp(scores - row_part[:, None]) + jnp.exp(scores - col_lse[None, :]))).astype(jnp.bfloat16)
        grouped = weights.reshape(-1, N_ROW, N_COL, ROWS_DEV).transpose(2, 0, 1, 3).reshape(N_COL, -1, N_ROW * ROWS_DEV)
        partials = jnp.einsum("cik,ckd->cid", grouped.astype(jnp.float32), passage_groups.astype(jnp.float32), precision=lax.Precision.HIGHEST)
        partials = lax.optimization_barrier(partials.astype(jnp.bfloat16)).astype(jnp.float32)
        query_part = partials.sum(axis=0)
        passage_part = jnp.dot(weights.T, query_rows, preferred_element_type=jnp.float32)
        passage_part = lax.optimization_barrier(passage_part.astype(jnp.bfloat16)).astype(jnp.float32)
        return passage_acc + passage_part, query_part

    passage_sum, query_sums = lax.scan(second_sweep, jnp.zeros((BATCH, EMBED), jnp.float32), (query_groups, row_lse))
    query_sum = query_sums.reshape(BATCH, EMBED)
    row_lse = row_lse.reshape(BATCH)
    paired_passage = passage[paired_index].astype(jnp.float32)
    positive_score = logit_scale * jnp.sum(query.astype(jnp.float32) * paired_passage, axis=1)
    loss_value = (jnp.sum(row_lse) + jnp.sum(col_lse) - 2.0 * jnp.sum(positive_score)) / (2.0 * BATCH)
    grad_query = (logit_scale * (query_sum - paired_passage)).astype(jnp.bfloat16)
    paired_query = jnp.zeros((BATCH, EMBED), jnp.float32).at[paired_index].set(query.astype(jnp.float32))
    grad_passage = (logit_scale * (passage_sum - paired_query)).astype(jnp.bfloat16)
    return (loss_value, grad_query, grad_passage)
```

```python
import jax
import jax.numpy as jnp
from jax import lax
from jax.sharding import Mesh, PartitionSpec as P

logit_scale = 20.0

AXES = ("yh", "x", "zh", "zl", "yl", "core")
SIZES = (4, 4, 4, 2, 2, 2)
PASS_AXES = ("x", "yl", "zl")
CHIP_AXES = ("yh", "zh")
QUERY_AXES = ("yh", "zh", "core")


def exchange(blocks, axes):
    return lax.all_to_all(blocks, axes, 0, 0, tiled=True)


def spread(x, n):
    return lax.optimization_barrier(jnp.broadcast_to(x[None], (n,) + x.shape))


def scores_of(q, p):
    return logit_scale * lax.dot_general(
        q, p, (((1,), (1,)), ((), ())), preferred_element_type=jnp.float32
    )


def lse(x, axis):
    peak = x.max(axis=axis)
    return peak + jnp.log(jnp.exp(x - jnp.expand_dims(peak, axis)).sum(axis=axis))


def local(query, passage, positive):
    rows, embed = query.shape
    n_pass = lax.axis_size(PASS_AXES)
    n_chip = lax.axis_size(CHIP_AXES)
    n_query = lax.axis_size(QUERY_AXES)
    n_p = n_pass * rows
    half = n_chip * rows
    core = lax.axis_index("core")
    swap = [(0, 1), (1, 0)]

    own = exchange(spread(query, n_chip), CHIP_AXES).reshape(half, embed)
    other = lax.ppermute(own, "core", swap)
    pall = exchange(spread(passage, n_pass), PASS_AXES).reshape(n_p, embed)

    slot = jnp.arange(rows, dtype=jnp.int32)
    onehot = (positive[0][:, None] == slot[None, :]).astype(jnp.bfloat16)
    paired_passage = jnp.dot(onehot, passage, preferred_element_type=jnp.float32)
    paired_query = lax.dot_general(
        onehot, query, (((0,), (0,)), ((), ())), preferred_element_type=jnp.float32
    )
    positive_sum = logit_scale * jnp.sum(query.astype(jnp.float32) * paired_passage)

    s0 = scores_of(own, pall)
    s1 = scores_of(other, pall)
    row0, row1 = lse(s0, 1), lse(s1, 1)
    col_peak = jnp.maximum(s0.max(axis=0), s1.max(axis=0))
    col_part = col_peak + jnp.log(
        jnp.exp(s0 - col_peak[None, :]).sum(axis=0) + jnp.exp(s1 - col_peak[None, :]).sum(axis=0)
    )

    col_all = exchange(spread(col_part.reshape(-1, 128), n_pass), PASS_AXES)
    col_lse = lse(col_all.reshape(n_pass, n_p), 0)

    first = jnp.where(core == 0, row0, row1)
    second = jnp.where(core == 0, row1, row0)
    lane = jnp.arange(128)
    extra = jnp.where(lane == 0, jnp.sum(col_lse), 0.0) + jnp.where(lane == 1, positive_sum, 0.0)
    extra = jnp.broadcast_to(extra[None], (8, 128))
    msg = jnp.concatenate([first.reshape(-1, 128), second.reshape(-1, 128), extra], axis=0)
    row_all = exchange(spread(msg, n_query), QUERY_AXES)
    k = half // 128
    row_can = lse(row_all[:, : 2 * k], 0).reshape(2, half)
    row_lse0 = jnp.where(core == 0, row_can[0], row_can[1])
    row_lse1 = jnp.where(core == 0, row_can[1], row_can[0])
    totals = row_all[:, 2 * k].sum(axis=0)
    side = jnp.sum(row_can) - 2.0 * totals[1]
    loss = (lax.psum(side, PASS_AXES) + totals[0]) / (2.0 * n_pass * n_query * rows)

    def weights(s, row_lse):
        return (0.5 * (jnp.exp(s - row_lse[:, None]) + jnp.exp(s - col_lse[None, :]))).astype(
            jnp.bfloat16
        )

    w1 = weights(s1, row_lse1)
    w0 = weights(s0, row_lse0)
    given = jnp.dot(w1, pall, preferred_element_type=jnp.float32).astype(jnp.bfloat16)
    taken = lax.ppermute(given, "core", swap)
    tn = (((0,), (0,)), ((), ()))
    pgrad = lax.dot_general(w0, own, tn, preferred_element_type=jnp.float32) + lax.dot_general(
        w1, other, tn, preferred_element_type=jnp.float32
    )
    pgrad = exchange(pgrad.astype(jnp.bfloat16).reshape(n_pass, rows, embed), PASS_AXES)
    qgrad = jnp.dot(w0, pall, preferred_element_type=jnp.float32) + taken.astype(jnp.float32)
    qgrad = exchange(qgrad.astype(jnp.bfloat16).reshape(n_chip, rows, embed), CHIP_AXES)

    query_sum = qgrad.astype(jnp.float32).sum(axis=0)
    passage_sum = pgrad.astype(jnp.float32).sum(axis=0)
    grad_query = (logit_scale * (query_sum - paired_passage)).astype(jnp.bfloat16)
    grad_passage = (logit_scale * (passage_sum - paired_query)).astype(jnp.bfloat16)
    return (loss, grad_query, grad_passage)


def solution(mesh):
    cut = Mesh(mesh.devices.reshape(SIZES), AXES)
    spec = P(AXES, None)
    return jax.shard_map(
        local,
        mesh=cut,
        in_specs=(spec, spec, spec),
        out_specs=(P(), spec, spec),
        check_vma=False,
    )
```

```python
import jax
import jax.numpy as jnp
from jax import lax
from jax.sharding import Mesh, PartitionSpec as P

logit_scale = 20.0

AXES = ("yh", "x", "zh", "zl", "yl", "core")
SIZES = (4, 4, 4, 2, 2, 2)
PASS_AXES = ("x", "zl", "yl")
NEAR_AXES = ("zl", "yl")
CHIP_AXES = ("yh", "zh")
LANES = 128


def exchange(blocks, axes):
    return lax.all_to_all(blocks, axes, 0, 0, tiled=True)


def spread(x, n):
    return lax.optimization_barrier(jnp.broadcast_to(x[None], (n,) + x.shape))


def swap_core(x):
    return lax.ppermute(x, "core", [(0, 1), (1, 0)])


def swap_near(x, m):
    n = lax.axis_size(NEAR_AXES)
    return lax.ppermute(x, NEAR_AXES, [(i, i ^ m) for i in range(n)])


def shift_x(x, d):
    n = lax.axis_size("x")
    return lax.ppermute(x, "x", [(i, (i + d) % n) for i in range(n)])


def scores_of(q, p):
    return logit_scale * lax.dot_general(
        q, p, (((1,), (1,)), ((), ())), preferred_element_type=jnp.float32
    )


def lse(x, axis):
    peak = x.max(axis=axis)
    return peak + jnp.log(jnp.exp(x - jnp.expand_dims(peak, axis)).sum(axis=axis))


def lse2(a, b):
    peak = jnp.maximum(a, b)
    return peak + jnp.log(jnp.exp(a - peak) + jnp.exp(b - peak))


def lanes_of(x, rows):
    hi = lax.reduce_precision(x, 8, 7)
    mid = lax.reduce_precision(x - hi, 8, 7)
    low = x - hi - mid
    lane = lax.broadcasted_iota(jnp.int32, (rows, LANES), 1)
    zero = jnp.zeros((rows, LANES), jnp.float32)
    return jnp.where(lane == 0, hi, jnp.where(lane == 1, mid, jnp.where(lane == 2, low, zero)))


def local(query, passage, positive):
    rows, embed = query.shape
    n_pass = lax.axis_size(PASS_AXES)
    n_x = lax.axis_size("x")
    n_near = lax.axis_size(NEAR_AXES)
    n_chip = lax.axis_size(CHIP_AXES)
    n_p = n_pass * rows
    half = n_chip * rows
    x_at = lax.axis_index("x")
    near_at = lax.axis_index(NEAR_AXES)

    own = exchange(spread(query, n_chip), CHIP_AXES).reshape(half, embed)
    near = jnp.concatenate([passage] + [swap_near(passage, m) for m in range(1, n_near)], axis=0)
    pall = jnp.concatenate([near] + [shift_x(near, n_x - d) for d in range(1, n_x)], axis=0)
    other = swap_core(own)

    slot = jnp.arange(rows, dtype=jnp.int32)
    onehot = (positive[0][:, None] == slot[None, :]).astype(jnp.bfloat16)
    paired_passage = jnp.dot(onehot, passage, preferred_element_type=jnp.float32)
    paired_query = lax.dot_general(
        onehot, query, (((0,), (0,)), ((), ())), preferred_element_type=jnp.float32
    )
    positive_sum = logit_scale * jnp.sum(query.astype(jnp.float32) * paired_passage)

    s0 = scores_of(own, pall)
    s1 = scores_of(other, pall)
    row0, row1 = lse(s0, 1), lse(s1, 1)
    rows_mine = jnp.concatenate([row0.reshape(-1, LANES), row1.reshape(-1, LANES)], axis=0)
    rows_theirs = swap_core(rows_mine)
    col_peak = jnp.maximum(s0.max(axis=0), s1.max(axis=0))
    col_part = col_peak + jnp.log(
        jnp.exp(s0 - col_peak[None, :]).sum(axis=0) + jnp.exp(s1 - col_peak[None, :]).sum(axis=0)
    )

    place = jnp.arange(n_pass, dtype=jnp.int32)
    source = (place // n_near - x_at + n_x) % n_x * n_near + (place % n_near ^ near_at)
    moved = source[:, None] == place[None, :]
    col_part = jnp.where(moved[:, :, None], col_part.reshape(1, n_pass, rows), 0.0).sum(axis=1)
    col_all = exchange(spread(col_part.reshape(-1, LANES), n_pass), PASS_AXES)
    col_lse = lse(col_all.reshape(n_pass, n_p), 0)
    col_lse = jnp.where(moved[:, :, None], col_lse.reshape(n_pass, 1, rows), 0.0).sum(axis=0)
    col_lse = col_lse.reshape(n_p)

    k = half // LANES
    pair = lse2(rows_mine, jnp.concatenate([rows_theirs[k:], rows_theirs[:k]], axis=0))
    lane = lax.broadcasted_iota(jnp.int32, (8, LANES), 1)
    extra = jnp.where(lane == 0, jnp.sum(col_lse), jnp.where(lane == 1, positive_sum, 0.0))
    row_all = exchange(spread(jnp.concatenate([pair, extra], axis=0), n_chip), CHIP_AXES)
    row_lse = lse(row_all[:, : 2 * k], 0)
    row_lse0, row_lse1 = row_lse[:k].reshape(half), row_lse[k:].reshape(half)
    totals = row_all[:, 2 * k].sum(axis=0)
    part = 0.5 * jnp.sum(row_lse) + totals[0] / n_pass - 2.0 * totals[1]

    def weights(s, row_lse):
        return (0.5 * (jnp.exp(s - row_lse[:, None]) + jnp.exp(s - col_lse[None, :]))).astype(
            jnp.bfloat16
        )

    w1 = weights(s1, row_lse1)
    w0 = weights(s0, row_lse0)
    given = jnp.dot(w1, pall, preferred_element_type=jnp.float32).astype(jnp.bfloat16)
    taken = swap_core(given)
    qgrad = jnp.dot(w0, pall, preferred_element_type=jnp.float32) + taken.astype(jnp.float32)
    qgrad = exchange(qgrad.astype(jnp.bfloat16).reshape(n_chip, rows, embed), CHIP_AXES)

    tn = (((0,), (0,)), ((), ()))
    pgrad = lax.dot_general(w0, own, tn, preferred_element_type=jnp.float32) + lax.dot_general(
        w1, other, tn, preferred_element_type=jnp.float32
    )
    pgrad = pgrad.reshape(n_x, n_near * rows, embed)

    def with_lanes(block, value):
        return jnp.concatenate([block, lanes_of(value, block.shape[0])], axis=1).astype(
            jnp.bfloat16
        )

    got = [shift_x(with_lanes(pgrad[d], part), d) for d in range(1, n_x)]
    mid = pgrad[0] + sum(g[:, :embed].astype(jnp.float32) for g in got)
    part = part + sum(g[0, embed:].astype(jnp.float32).sum() for g in got)
    mid = mid.reshape(n_near, rows, embed)
    got = [swap_near(with_lanes(mid[m], part), m) for m in range(1, n_near)]
    passage_sum = mid[0] + sum(g[:, :embed].astype(jnp.float32) for g in got)
    part = part + sum(g[0, embed:].astype(jnp.float32).sum() for g in got)
    part = part + swap_core(jnp.broadcast_to(part, (8, LANES)))[0, 0]
    loss = part / (2.0 * n_pass * n_chip * 2 * rows)

    query_sum = qgrad.astype(jnp.float32).sum(axis=0)
    grad_query = (logit_scale * (query_sum - paired_passage)).astype(jnp.bfloat16)
    grad_passage = (logit_scale * (passage_sum - paired_query)).astype(jnp.bfloat16)
    return (loss, grad_query, grad_passage)


def solution(mesh):
    cut = Mesh(mesh.devices.reshape(SIZES), AXES)
    spec = P(AXES, None)
    return jax.shard_map(
        local,
        mesh=cut,
        in_specs=(spec, spec, spec),
        out_specs=(P(), spec, spec),
        check_vma=False,
    )
```

```python
import jax
import jax.numpy as jnp
from jax import lax
from jax.sharding import Mesh, PartitionSpec as P


logit_scale = 20.0

AXES = ("yh", "x", "z", "yl", "core")
SIZES = (4, 4, 8, 2, 2)
PASS_AXES = ("x", "yh")
CHIP_AXES = ("z", "yl")
LANES = 128


def exchange(blocks, axes):
    return lax.all_to_all(blocks, axes, 0, 0, tiled=True)


def spread(x, n):
    return lax.optimization_barrier(jnp.broadcast_to(x[None], (n,) + x.shape))


def swap_core(x):
    return lax.ppermute(x, "core", [(0, 1), (1, 0)])


def shift_x(x, d):
    n = lax.axis_size("x")
    return lax.ppermute(x, "x", [(i, (i + d) % n) for i in range(n)])


def scores_of(q, p):
    return logit_scale * lax.dot_general(
        q, p, (((1,), (1,)), ((), ())), preferred_element_type=jnp.float32
    )


def lse(x, axis):
    peak = x.max(axis=axis)
    return peak + jnp.log(jnp.exp(x - jnp.expand_dims(peak, axis)).sum(axis=axis))


def lse2(a, b):
    peak = jnp.maximum(a, b)
    return peak + jnp.log(jnp.exp(a - peak) + jnp.exp(b - peak))


def lanes_of(x, rows):
    hi = lax.reduce_precision(x, 8, 7)
    mid = lax.reduce_precision(x - hi, 8, 7)
    low = x - hi - mid
    lane = lax.broadcasted_iota(jnp.int32, (rows, LANES), 1)
    zero = jnp.zeros((rows, LANES), jnp.float32)
    return jnp.where(lane == 0, hi, jnp.where(lane == 1, mid, jnp.where(lane == 2, low, zero)))


def inner(query, passage, positive):
    rows, embed = query.shape
    n_pass = lax.axis_size(PASS_AXES)
    n_x = lax.axis_size("x")
    n_yh = lax.axis_size("yh")
    n_chip = lax.axis_size(CHIP_AXES)
    n_p = n_pass * rows
    half = n_chip * rows
    x_at = lax.axis_index("x")

    near = exchange(spread(passage, n_yh), "yh").reshape(n_yh * rows, embed)
    own = exchange(spread(query, n_chip), CHIP_AXES).reshape(half, embed)
    far = [shift_x(near, n_x - d) for d in range(1, n_x)]
    pall = lax.optimization_barrier(jnp.concatenate([near] + far, axis=0))
    other = swap_core(own)

    slot = jnp.arange(rows, dtype=jnp.int32)
    onehot = (positive[0][:, None] == slot[None, :]).astype(jnp.bfloat16)
    paired_passage = jnp.dot(onehot, passage, preferred_element_type=jnp.float32)
    paired_query = lax.dot_general(
        onehot, query, (((0,), (0,)), ((), ())), preferred_element_type=jnp.float32
    )
    positive_sum = logit_scale * jnp.sum(query.astype(jnp.float32) * paired_passage)

    s0 = scores_of(own, pall)
    s1 = scores_of(other, pall)
    row0, row1 = lse(s0, 1), lse(s1, 1)
    rows_mine = jnp.concatenate([row0.reshape(-1, LANES), row1.reshape(-1, LANES)], axis=0)
    rows_theirs = swap_core(rows_mine)
    col_peak = jnp.maximum(s0.max(axis=0), s1.max(axis=0))
    col_part = col_peak + jnp.log(
        jnp.exp(s0 - col_peak[None, :]).sum(axis=0) + jnp.exp(s1 - col_peak[None, :]).sum(axis=0)
    )

    place = jnp.arange(n_x, dtype=jnp.int32)
    moved = ((place[:, None] - x_at + n_x) % n_x == place[None, :])[:, :, None]
    col_part = jnp.where(moved, col_part.reshape(1, n_x, n_yh * rows), 0.0).sum(axis=1)
    col_all = exchange(spread(col_part.reshape(-1, LANES), n_pass), PASS_AXES)
    col_lse = lse(col_all, 0).reshape(n_x, 1, n_yh * rows)
    col_lse = jnp.where(moved, col_lse, 0.0).sum(axis=0).reshape(n_p)

    k = half // LANES
    pair = lse2(rows_mine, jnp.concatenate([rows_theirs[k:], rows_theirs[:k]], axis=0))
    lane = lax.broadcasted_iota(jnp.int32, (8, LANES), 1)
    extra = jnp.where(lane == 0, jnp.sum(col_lse), jnp.where(lane == 1, positive_sum, 0.0))
    row_all = exchange(spread(jnp.concatenate([pair, extra], axis=0), n_chip), CHIP_AXES)
    row_lse = lse(row_all[:, : 2 * k], 0)
    row_lse0, row_lse1 = row_lse[:k].reshape(half), row_lse[k:].reshape(half)
    totals = row_all[:, 2 * k].sum(axis=0)
    part = 0.5 * jnp.sum(row_lse) + totals[0] / n_pass - 2.0 * totals[1]

    def weights(s, row_lse):
        return (0.5 * (jnp.exp(s - row_lse[:, None]) + jnp.exp(s - col_lse[None, :]))).astype(
            jnp.bfloat16
        )

    w1 = weights(s1, row_lse1)
    w0 = weights(s0, row_lse0)
    given = jnp.dot(w1, pall, preferred_element_type=jnp.float32).astype(jnp.bfloat16)
    taken = swap_core(given)
    qgrad = jnp.dot(w0, pall, preferred_element_type=jnp.float32) + taken.astype(jnp.float32)
    qgrad = exchange(qgrad.astype(jnp.bfloat16).reshape(n_chip, rows, embed), CHIP_AXES)

    tn = (((0,), (0,)), ((), ()))
    pgrad = lax.dot_general(w0, own, tn, preferred_element_type=jnp.float32) + lax.dot_general(
        w1, other, tn, preferred_element_type=jnp.float32
    )
    pgrad = pgrad.reshape(n_x, n_yh * rows, embed)

    def with_lanes(block, value):
        return jnp.concatenate([block, lanes_of(value, block.shape[0])], axis=1).astype(
            jnp.bfloat16
        )

    got = [shift_x(with_lanes(pgrad[d], part), d) for d in range(1, n_x)]
    mid = pgrad[0] + sum(g[:, :embed].astype(jnp.float32) for g in got)
    part = part + sum(g[0, embed:].astype(jnp.float32).sum() for g in got)
    part = part + swap_core(jnp.broadcast_to(part, (8, LANES)))[0, 0]
    mid = exchange(with_lanes(mid, part).reshape(n_yh, rows, embed + LANES), "yh")
    passage_sum = mid[:, :, :embed].astype(jnp.float32).sum(axis=0)
    part = mid[:, 0, embed:].astype(jnp.float32).sum()
    loss = part / (2.0 * n_pass * n_chip * 2 * rows)

    query_sum = qgrad.astype(jnp.float32).sum(axis=0)
    grad_query = (logit_scale * (query_sum - paired_passage)).astype(jnp.bfloat16)
    grad_passage = (logit_scale * (passage_sum - paired_query)).astype(jnp.bfloat16)
    return (loss, grad_query, grad_passage)


def solution(mesh):
    cut = Mesh(mesh.devices.reshape(SIZES), AXES)
    spec = P(AXES, None)
    return jax.shard_map(
        inner,
        mesh=cut,
        in_specs=(spec, spec, spec),
        out_specs=(P(), spec, spec),
        check_vma=False,
    )
```

```python
import jax
import jax.numpy as jnp
from jax import lax
from jax.sharding import Mesh, PartitionSpec as P


logit_scale = 20.0

AXES = ("yh", "x", "z", "yl", "core")
SIZES = (4, 4, 8, 2, 2)
PASS_AXES = ("x", "yh")
CHIP_AXES = ("z", "yl")
LANES = 128


def exchange(blocks, axes):
    return lax.all_to_all(blocks, axes, 0, 0, tiled=True)


def spread(x, n):
    return lax.optimization_barrier(jnp.broadcast_to(x[None], (n,) + x.shape))


def swap_core(x):
    return lax.ppermute(x, "core", [(0, 1), (1, 0)])


def shift_x(x, d):
    n = lax.axis_size("x")
    return lax.ppermute(x, "x", [(i, (i + d) % n) for i in range(n)])


def scores_of(q, p):
    return logit_scale * lax.dot_general(
        q, p, (((1,), (1,)), ((), ())), preferred_element_type=jnp.float32
    )


def lse(x, axis):
    peak = x.max(axis=axis)
    return peak + jnp.log(jnp.exp(x - jnp.expand_dims(peak, axis)).sum(axis=axis))


def lse2(a, b):
    peak = jnp.maximum(a, b)
    return peak + jnp.log(jnp.exp(a - peak) + jnp.exp(b - peak))


def add_partner(x, axis, step):
    n = lax.axis_size(axis)
    return x + lax.ppermute(x, axis, [(i, i ^ step) for i in range(n)])


def inner(query, passage, positive):
    rows, embed = query.shape
    n_pass = lax.axis_size(PASS_AXES)
    n_x = lax.axis_size("x")
    n_yh = lax.axis_size("yh")
    n_chip = lax.axis_size(CHIP_AXES)
    n_p = n_pass * rows
    half = n_chip * rows
    x_at = lax.axis_index("x")

    near = exchange(spread(passage, n_yh), "yh").reshape(n_yh * rows, embed)
    own = exchange(spread(query, n_chip), CHIP_AXES).reshape(half, embed)
    far = [shift_x(near, n_x - d) for d in range(1, n_x)]
    ring = jnp.stack([near] + far + [near] + far[:-1])
    pall = lax.dynamic_slice_in_dim(ring, (n_x - x_at) % n_x, n_x, 0)
    pall = lax.optimization_barrier(pall.reshape(n_p, embed))
    other = swap_core(own)

    slot = jnp.arange(rows, dtype=jnp.int32)
    onehot = (positive[0][:, None] == slot[None, :]).astype(jnp.bfloat16)
    paired_passage = jnp.dot(onehot, passage, preferred_element_type=jnp.float32)
    paired_query = lax.dot_general(
        onehot, query, (((0,), (0,)), ((), ())), preferred_element_type=jnp.float32
    )
    positive_sum = logit_scale * jnp.sum(query.astype(jnp.float32) * paired_passage)

    s0 = scores_of(own, pall)
    s1 = scores_of(other, pall)
    row0, row1 = lse(s0, 1), lse(s1, 1)
    rows_mine = jnp.concatenate([row0.reshape(-1, LANES), row1.reshape(-1, LANES)], axis=0)
    rows_theirs = swap_core(rows_mine)
    col_peak = jnp.maximum(s0.max(axis=0), s1.max(axis=0))
    col_part = col_peak + jnp.log(
        jnp.exp(s0 - col_peak[None, :]).sum(axis=0) + jnp.exp(s1 - col_peak[None, :]).sum(axis=0)
    )

    col_all = exchange(spread(col_part.reshape(-1, LANES), n_pass), PASS_AXES)
    col_lse = lse(col_all, 0).reshape(n_p)

    k = half // LANES
    pair = lse2(rows_mine, jnp.concatenate([rows_theirs[k:], rows_theirs[:k]], axis=0))
    lane = lax.broadcasted_iota(jnp.int32, (8, LANES), 1)
    extra = jnp.where(lane == 0, jnp.sum(col_lse), jnp.where(lane == 1, positive_sum, 0.0))
    row_all = exchange(spread(jnp.concatenate([pair, extra], axis=0), n_chip), CHIP_AXES)
    row_lse = lse(row_all[:, : 2 * k], 0)
    row_lse0, row_lse1 = row_lse[:k].reshape(half), row_lse[k:].reshape(half)
    totals = row_all[:, 2 * k].sum(axis=0)
    part = 0.5 * jnp.sum(row_lse) + totals[0] / n_pass - 2.0 * totals[1]

    def weights(s, row_lse):
        return (0.5 * (jnp.exp(s - row_lse[:, None]) + jnp.exp(s - col_lse[None, :]))).astype(
            jnp.bfloat16
        )

    w1 = weights(s1, row_lse1)
    w0 = weights(s0, row_lse0)
    tn = (((0,), (0,)), ((), ()))
    pgrad = lax.dot_general(w0, own, tn, preferred_element_type=jnp.float32) + lax.dot_general(
        w1, other, tn, preferred_element_type=jnp.float32
    )
    pgrad = exchange(pgrad.astype(jnp.bfloat16).reshape(n_pass, rows, embed), PASS_AXES)
    given = jnp.dot(w1, pall, preferred_element_type=jnp.float32).astype(jnp.bfloat16)
    taken = swap_core(given)
    qgrad = jnp.dot(w0, pall, preferred_element_type=jnp.float32) + taken.astype(jnp.float32)
    qgrad = qgrad.astype(jnp.bfloat16)
    qgrad = exchange(qgrad.reshape(n_chip, rows, embed), CHIP_AXES)
    part = add_partner(jnp.broadcast_to(part, (8, LANES)), "core", 1)
    part = add_partner(part, "x", 1)
    part = add_partner(part, "x", 2)
    part = add_partner(part, "yh", 1)
    part = add_partner(part, "yh", 2)
    loss = part[0, 0] / (2.0 * n_pass * n_chip * 2 * rows)

    passage_sum = pgrad.astype(jnp.float32).sum(axis=0)
    query_sum = qgrad.astype(jnp.float32).sum(axis=0)
    grad_query = (logit_scale * (query_sum - paired_passage)).astype(jnp.bfloat16)
    grad_passage = (logit_scale * (passage_sum - paired_query)).astype(jnp.bfloat16)
    return (loss, grad_query, grad_passage)


def solution(mesh):
    cut = Mesh(mesh.devices.reshape(SIZES), AXES)
    spec = P(AXES, None)
    return jax.shard_map(
        inner,
        mesh=cut,
        in_specs=(spec, spec, spec),
        out_specs=(P(), spec, spec),
        check_vma=False,
    )
```

```python
import jax
import jax.numpy as jnp
from jax import lax
from jax.sharding import Mesh, PartitionSpec as P


logit_scale = 20.0

AXES = ("yh", "x", "z", "yl", "core")
SIZES = (4, 4, 8, 2, 2)
PASS_AXES = ("x", "yh")
CHIP_AXES = ("z", "yl")
LANES = 128


def exchange(blocks, axes):
    return lax.all_to_all(blocks, axes, 0, 0, tiled=True)


def spread(x, n):
    return lax.optimization_barrier(jnp.broadcast_to(x[None], (n,) + x.shape))


def swap_core(x):
    return lax.ppermute(x, "core", [(0, 1), (1, 0)])


def shift_x(x, d):
    n = lax.axis_size("x")
    return lax.ppermute(x, "x", [(i, (i + d) % n) for i in range(n)])


def scores_of(q, p):
    return logit_scale * lax.dot_general(
        q, p, (((1,), (1,)), ((), ())), preferred_element_type=jnp.float32
    )


def lse(x, axis):
    peak = x.max(axis=axis)
    return peak + jnp.log(jnp.exp(x - jnp.expand_dims(peak, axis)).sum(axis=axis))


def lse2(a, b):
    peak = jnp.maximum(a, b)
    return peak + jnp.log(jnp.exp(a - peak) + jnp.exp(b - peak))


def add_partner(x, axis, step):
    n = lax.axis_size(axis)
    return x + lax.ppermute(x, axis, [(i, i ^ step) for i in range(n)])


def inner(query, passage, positive):
    rows, embed = query.shape
    n_pass = lax.axis_size(PASS_AXES)
    n_x = lax.axis_size("x")
    n_yh = lax.axis_size("yh")
    n_chip = lax.axis_size(CHIP_AXES)
    n_p = n_pass * rows
    half = n_chip * rows
    x_at = lax.axis_index("x")

    near = exchange(spread(passage, n_yh), "yh").reshape(n_yh * rows, embed)
    own = exchange(spread(query, n_chip), CHIP_AXES).reshape(half, embed)
    far = [shift_x(near, n_x - d) for d in range(1, n_x)]
    pall = jnp.zeros((n_x, n_yh * rows, embed), query.dtype)
    for d, block in enumerate([near] + far):
        pall = lax.dynamic_update_slice_in_dim(pall, block[None], (x_at + d) % n_x, 0)
    pall = lax.optimization_barrier(pall.reshape(n_p, embed))
    other = swap_core(own)

    slot = jnp.arange(rows, dtype=jnp.int32)
    onehot = (positive[0][:, None] == slot[None, :]).astype(jnp.bfloat16)
    paired_passage = jnp.dot(onehot, passage, preferred_element_type=jnp.float32)
    paired_query = lax.dot_general(
        onehot, query, (((0,), (0,)), ((), ())), preferred_element_type=jnp.float32
    )
    positive_sum = logit_scale * jnp.sum(query.astype(jnp.float32) * paired_passage)

    s0 = scores_of(own, pall)
    s1 = scores_of(other, pall)
    row0, row1 = lse(s0, 1), lse(s1, 1)
    rows_mine = jnp.concatenate([row0.reshape(-1, LANES), row1.reshape(-1, LANES)], axis=0)
    rows_theirs = swap_core(rows_mine)
    col_peak = jnp.maximum(s0.max(axis=0), s1.max(axis=0))
    col_part = col_peak + jnp.log(
        jnp.exp(s0 - col_peak[None, :]).sum(axis=0) + jnp.exp(s1 - col_peak[None, :]).sum(axis=0)
    )

    col_all = exchange(spread(col_part.reshape(-1, LANES), n_pass), PASS_AXES)
    col_lse = lse(col_all, 0).reshape(n_p)

    k = half // LANES
    pair = lse2(rows_mine, jnp.concatenate([rows_theirs[k:], rows_theirs[:k]], axis=0))
    lane = lax.broadcasted_iota(jnp.int32, (8, LANES), 1)
    extra = jnp.where(lane == 0, jnp.sum(col_lse), jnp.where(lane == 1, positive_sum, 0.0))
    row_all = exchange(spread(jnp.concatenate([pair, extra], axis=0), n_chip), CHIP_AXES)
    row_lse = lse(row_all[:, : 2 * k], 0)
    row_lse0, row_lse1 = row_lse[:k].reshape(half), row_lse[k:].reshape(half)
    totals = row_all[:, 2 * k].sum(axis=0)
    part = 0.5 * jnp.sum(row_lse) + totals[0] / n_pass - 2.0 * totals[1]

    def weights(s, row_lse):
        return (0.5 * (jnp.exp(s - row_lse[:, None]) + jnp.exp(s - col_lse[None, :]))).astype(
            jnp.bfloat16
        )

    w1 = weights(s1, row_lse1)
    w0 = weights(s0, row_lse0)
    tn = (((0,), (0,)), ((), ()))
    pgrad = lax.dot_general(w0, own, tn, preferred_element_type=jnp.float32) + lax.dot_general(
        w1, other, tn, preferred_element_type=jnp.float32
    )
    pgrad = exchange(pgrad.astype(jnp.bfloat16).reshape(n_pass, rows, embed), PASS_AXES)
    given = jnp.dot(w1, pall, preferred_element_type=jnp.float32).astype(jnp.bfloat16)
    taken = swap_core(given)
    qgrad = jnp.dot(w0, pall, preferred_element_type=jnp.float32) + taken.astype(jnp.float32)
    qgrad = qgrad.astype(jnp.bfloat16)
    qgrad = exchange(qgrad.reshape(n_chip, rows, embed), CHIP_AXES)
    part = add_partner(jnp.broadcast_to(part, (8, LANES)), "core", 1)
    part = add_partner(part, "x", 1)
    part = add_partner(part, "x", 2)
    part = add_partner(part, "yh", 1)
    part = add_partner(part, "yh", 2)
    loss = part[0, 0] / (2.0 * n_pass * n_chip * 2 * rows)

    passage_sum = pgrad.astype(jnp.float32).sum(axis=0)
    query_sum = qgrad.astype(jnp.float32).sum(axis=0)
    grad_query = (logit_scale * (query_sum - paired_passage)).astype(jnp.bfloat16)
    grad_passage = (logit_scale * (passage_sum - paired_query)).astype(jnp.bfloat16)
    return (loss, grad_query, grad_passage)


def solution(mesh):
    cut = Mesh(mesh.devices.reshape(SIZES), AXES)
    spec = P(AXES, None)
    return jax.shard_map(
        inner,
        mesh=cut,
        in_specs=(spec, spec, spec),
        out_specs=(P(), spec, spec),
        check_vma=False,
    )
```
